32 devices in a mesh: harm: 4 (over z), tx: 4 (over y, x), ty: 2 (over core).
Axes of the slice: x: 2, y: 2, z: 4, core: 2. Of those that a mesh axis runs over, the one named last changes fastest.
Arguments:
- wave_spectrum: float32 [2, 512, 16, 256], P(None, 'harm', 'tx', 'ty'), may hold values from -6 to 6
- lens_window: int32 [16, 256], P('tx', 'ty'), may hold values 0 or 1
- medium_label: int32 [16, 256], P('tx', 'ty'), may hold values from 0 to 7
- thermal_excess_prior: float32 [16, 256], P('tx', 'ty'), may hold values from -6 to 6
- attenuation_by_kind: float32 [8], replicated, may hold values from 0.2 to 2
- blood_drain_by_kind: float32 [8], replicated, may hold values from 0.02 to 0.2
- diffusivity_by_kind: float32 [8], replicated, may hold values from 0.04 to 0.22
Outputs:
- field_out: float32 [2, 512, 16, 256], P(None, 'harm', 'tx', 'ty')
- thermal_excess_later: float32 [16, 256], P('tx', 'ty')
The draws below stay inside these ranges and needn't reach their ends.
All inputs are finite; a program needn't handle non-finite values. No bound on the sum of `lens_window` on one device may be relied on, other than what follows from the above.
Results may differ from the reference program's by a relative error of at most 0.000071.
Values sent between devices are 32-bit elements; how exact they have to be, the bound alone decides.
No kernel may reach another device: no remote copies, remote signals or barrier semaphores. Data moves between devices by JAX's collectives and lax.ppermute only.
A program may use at most 64 MiB of HBM per device.

```python
import math
import jax
import jax.numpy as jnp
from jax import lax

HARM = 512
CYCLE_READINGS = 2048
NCLASS = 8
CELLS_LEADING = 16
CELLS_TRAILING = 256


def set_ends(array, rng, smallest, top_value):
    index_at = [jax.random.randint(jax.random.fold_in(rng, axis), (), 0, length) for axis, length in enumerate(array.shape)]
    main_axis = array.shape.index(max(array.shape))
    beside = index_at[:main_axis] + [(index_at[main_axis] + 1) % array.shape[main_axis]] + index_at[main_axis + 1:]
    return array.at[tuple(index_at)].set(smallest).at[tuple(beside)].set(top_value)


def shard_levels(stream_key, extent, pieces, least, high):
    def one(dim, shards_of):
        heights = jax.random.uniform(jax.random.fold_in(jax.random.fold_in(stream_key, 6), dim), (shards_of,), jnp.float32, least / len(pieces), high / len(pieces))
        return jnp.repeat(jnp.exp(heights), extent[dim] // shards_of).reshape((-1,) + (1,) * (len(extent) - dim - 1))

    level = one(*pieces[0])
    for cut in pieces[1:]:
        level = level * one(*cut)
    return level


def normal_values(key, dims, width, limit, pieces=(), kind=jnp.bfloat16):
    drawn = width * jax.random.normal(key, dims, jnp.float32)
    if pieces:
        drawn = drawn * shard_levels(key, dims, pieces, -0.22, 0.18)
    return jnp.clip(drawn, -limit, limit).astype(kind)


def setup_inputs(seed: int = 0) -> dict:
    streams_of = jax.random.split(jax.random.key(seed), 8)
    wave_spectrum = normal_values(streams_of[0], (2, HARM, CELLS_LEADING, CELLS_TRAILING), 1.0, 6.0, ((1, 4), (2, 4), (3, 2)), jnp.float32)
    lens_window = set_ends((jax.random.randint(streams_of[1], (CELLS_LEADING, CELLS_TRAILING), 0, 3) < 2).astype(jnp.int32), jax.random.fold_in(streams_of[1], 1), 0, 1)
    medium_label = set_ends(jax.random.randint(streams_of[2], (CELLS_LEADING, CELLS_TRAILING), 0, NCLASS), jax.random.fold_in(streams_of[2], 1), 0, NCLASS - 1).astype(jnp.int32)
    thermal_excess_prior = normal_values(streams_of[3], (CELLS_LEADING, CELLS_TRAILING), 1.0, 6.0, ((0, 4), (1, 2)), jnp.float32)
    attenuation_by_kind = jnp.clip(jnp.exp(jax.random.uniform(streams_of[4], (NCLASS,), jnp.float32, math.log(0.2), math.log(2.0))), 0.2, 2.0)
    blood_drain_by_kind = jnp.clip(jnp.exp(jax.random.uniform(streams_of[5], (NCLASS,), jnp.float32, math.log(0.02), math.log(0.2))), 0.02, 0.2)
    diffusivity_by_kind = jnp.clip(jnp.exp(jax.random.uniform(streams_of[6], (NCLASS,), jnp.float32, math.log(0.04), math.log(0.22))), 0.04, 0.22)
    return {"wave_spectrum": wave_spectrum, "lens_window": lens_window, "medium_label": medium_label, "thermal_excess_prior": thermal_excess_prior, "attenuation_by_kind": attenuation_by_kind, "blood_drain_by_kind": blood_drain_by_kind, "diffusivity_by_kind": diffusivity_by_kind}


diffraction_gain = 0.3
nonlinear_gain = 0.3

def laplace(padded):
    center = padded[..., 1:-1, 1:-1]
    return padded[..., 2:, 1:-1] + padded[..., :-2, 1:-1] + padded[..., 1:-1, 2:] + padded[..., 1:-1, :-2] - 4.0 * center

def pad_plane(values):
    widths = [(0, 0)] * (values.ndim - 2) + [(1, 1), (1, 1)]
    return jnp.pad(values, widths)

def build_table(overall):
    moment_grid = jnp.arange(CYCLE_READINGS, dtype=jnp.int32)
    overtone_series = jnp.arange(1, overall + 1, dtype=jnp.int32)
    cycle_argument = moment_grid[:, None] * overtone_series[None, :] % CYCLE_READINGS
    angle = 2.0 * math.pi / CYCLE_READINGS * cycle_argument.astype(jnp.float32)
    return jnp.concatenate([jnp.cos(angle), -jnp.sin(angle)], axis=1)

def reference(wave_spectrum, lens_window, medium_label, thermal_excess_prior, attenuation_by_kind, blood_drain_by_kind, diffusivity_by_kind):
    orders = jnp.arange(1, HARM + 1, dtype=jnp.int32).astype(jnp.float32)
    weight = 0.25 + 0.75 * lens_window.astype(jnp.float32)
    source = wave_spectrum * weight
    block_size = 32 if HARM % 32 == 0 else HARM
    groups = HARM // block_size
    blocked = jnp.moveaxis(source.reshape(2, groups, block_size, CELLS_LEADING, CELLS_TRAILING), 1, 0)
    gains = (diffraction_gain / orders).reshape(groups, block_size, 1, 1)

    def diffract(pair):
        anchor, gain_rate = pair
        current = anchor
        for scale_divider in (4.0, 3.0, 2.0, 1.0):
            bending = gain_rate * laplace(pad_plane(current))
            current = anchor + 1.0 / scale_divider * jnp.stack([-bending[1], bending[0]])
        return current
    advanced = lax.map(diffract, (blocked, gains))
    advanced = jnp.moveaxis(advanced, 0, 1).reshape(2, HARM, CELLS_LEADING, CELLS_TRAILING)
    dft_table = build_table(HARM)
    scale_synth = HARM ** (-0.5)
    scale_analysis = 2.0 * math.sqrt(HARM) / CYCLE_READINGS
    rate = nonlinear_gain / HARM * orders[:, None]
    row_major = jnp.moveaxis(advanced, 2, 0)

    def nonlinear(row_block):
        stacked = row_block.reshape(2 * HARM, CELLS_TRAILING)
        pressure = scale_synth * jnp.dot(dft_table, stacked, precision=lax.Precision.HIGHEST)
        spectrum = scale_analysis * lax.dot_general(dft_table, pressure * pressure, (((0,), (0,)), ((), ())), precision=lax.Precision.HIGHEST)
        real_new = stacked[:HARM] - rate * spectrum[HARM:]
        imag_new = stacked[HARM:] + rate * spectrum[:HARM]
        return jnp.stack([real_new, imag_new])
    updated = lax.map(nonlinear, row_major)
    field_out = jnp.moveaxis(updated, 0, 2)
    heat = lax.optimization_barrier(jnp.sum(orders[:, None, None] * (field_out[0] * field_out[0] + field_out[1] * field_out[1]), axis=0))
    codes = jnp.arange(NCLASS, dtype=jnp.int32)
    onehot = (medium_label[None, :, :] == codes[:, None, None]).astype(jnp.float32)
    absorb_map = lax.optimization_barrier(jnp.sum(attenuation_by_kind[:, None, None] * onehot, axis=0))
    conduct_map = lax.optimization_barrier(jnp.sum(diffusivity_by_kind[:, None, None] * onehot, axis=0))
    perfuse_map = lax.optimization_barrier(jnp.sum(blood_drain_by_kind[:, None, None] * onehot, axis=0))
    deposit = absorb_map * heat / (HARM * HARM)
    thermal_excess_later = thermal_excess_prior
    for repeat in range(4):
        thermal_excess_later = thermal_excess_later + conduct_map * laplace(pad_plane(thermal_excess_later)) - perfuse_map * thermal_excess_later + deposit
    return (field_out, thermal_excess_later)
```

```python
import functools
import math

import jax
import jax.numpy as jnp
import numpy as np
from jax import lax
from jax.experimental import pallas as pl
from jax.experimental.pallas import tpu as pltpu
from jax.sharding import PartitionSpec as P

CYCLE_READINGS = 2048
diffraction_gain = 0.3
nonlinear_gain = 0.3
ORDER = 4
STRIP = 2 * ORDER

VMEM = pl.BlockSpec(memory_space=pltpu.VMEM)
SMEM = pl.BlockSpec(memory_space=pltpu.SMEM)


def call(kernel, args, outs, scratch=(), name=None):
    return pl.pallas_call(
        kernel,
        out_shape=outs,
        in_specs=[SMEM] + [VMEM] * (len(args) - 1),
        out_specs=jax.tree.map(lambda _: VMEM, outs),
        scratch_shapes=scratch,
        name=name,
    )(*args)


def f32(*shape):
    return jax.ShapeDtypeStruct(shape, jnp.float32)


def swap(block, axis, k):
    count = lax.axis_size(axis)
    return lax.ppermute(block, axis, [(i, i ^ k) for i in range(count)])


def first_harmonic(h, q, own, hq, half):
    return h * own + 1 + q // half + 2 * lax.rem(q, half) * hq


def spread_kernel(where, wave, lens, *outs):
    tx = where[1]
    parts = len(outs)
    half = parts // 2
    height, _, hq, _ = outs[0].shape
    weight = 0.25 + 0.75 * lens[...].astype(jnp.float32)
    for k, out in enumerate(outs):
        q = tx ^ k
        start = (q // half + 2 * lax.rem(q, half) * hq) * height
        for r in range(height):
            w = weight[r : r + 1, :]
            for c in range(2):
                out[r, c] = wave[c, pl.ds(start + r, hq, stride=2 * height), :] * w


def strip_kernel(where, *refs):
    *blocks, plane, strips = refs
    tx = where[1]
    height, _, hq, _ = blocks[0].shape
    rows, _, _, breadth = plane.shape
    for k, block in enumerate(blocks):
        base = (tx ^ k) * height
        for r in range(height):
            plane[base + r] = block[r]
    per = breadth // STRIP
    lane = lax.broadcasted_iota(jnp.int32, (hq, breadth), 1) // STRIP
    for t in range(strips.shape[0]):
        for c in range(2):
            packed = jnp.zeros((hq, breadth), jnp.float32)
            for i in range(min(per, rows - t * per)):
                rolled = pltpu.roll(plane[t * per + i, c], STRIP * i + ORDER, 1)
                packed = jnp.where(lane == i, rolled, packed)
            strips[t, c] = packed


def bend_kernel(tx_count, ty_count, own, where, plane, *refs):
    *strips, out = refs
    h, tx, ty = where[0], where[1], where[2]
    rows, _, hq, breadth = plane.shape
    harm_count = out.shape[0] // tx_count
    height = rows // tx_count
    per = breadth // STRIP
    lane = lax.broadcasted_iota(jnp.int32, (8, breadth), 1)
    right_side = (lane < ORDER) & (ty < ty_count - 1)
    left_side = (lane >= breadth - ORDER) & (ty > 0)
    side = (right_side | left_side)[None]
    first = (lane == 0)[None]
    last = (lane == breadth - 1)[None]
    low = first_harmonic(h, tx, own, hq, tx_count // 2)
    inner = lax.broadcasted_iota(jnp.int32, (8, breadth), 0)
    zero = jnp.zeros((1, 8, breadth), jnp.float32)

    def beside(m, b):
        m1, b1 = pltpu.roll(m, breadth - 1, 2), pltpu.roll(b, breadth - 1, 2)
        m2, b2 = pltpu.roll(m, 1, 2), pltpu.roll(b, 1, 2)
        return (
            jnp.where(last, b1, m1) + jnp.where(first, b2, m2),
            jnp.where(last, m1, b1) + jnp.where(first, m2, b2),
        )

    def laplace(m, b):
        m_side, b_side = beside(m, b)
        out = []
        for v, s in ((m, m_side), (b, b_side)):
            near = jnp.concatenate([v[1:], zero], 0) + jnp.concatenate([zero, v[:-1]], 0)
            out.append(near + s - 4.0 * v)
        return out

    def group(g, carry):
        at = pl.multiple_of(g * 8, 8)
        orders = (low + 2 * (at + inner)).astype(jnp.float32)
        gain = diffraction_gain / orders
        source = []
        for c in range(2):
            main = plane[:, c, pl.ds(at, 8), :]
            edge = []
            for row in range(rows):
                t, i = divmod(row, per)
                back = (-(STRIP * i + ORDER)) % breadth
                if len(strips) == 1:
                    piece = strips[0][t, c, pl.ds(at, 8), :]
                    edge.append(pltpu.roll(piece, back, 1)[None])
                else:
                    from_left = pltpu.roll(strips[0][t, c, pl.ds(at, 8), :], back, 1)
                    from_right = pltpu.roll(strips[1][t, c, pl.ds(at, 8), :], back, 1)
                    edge.append(jnp.where(lane < ORDER, from_right, from_left)[None])
            source.append((main, jnp.where(side, jnp.concatenate(edge, 0), 0.0)))
        (re0, rb0), (im0, ib0) = source
        re, rb, im, ib = re0, rb0, im0, ib0
        for divider in (4.0, 3.0, 2.0, 1.0):
            rate = (gain * (1.0 / divider))[None]
            lre, lrb = laplace(re, rb)
            lim, lib = laplace(im, ib)
            re, im = re0 - rate * lim, im0 + rate * lre
            rb = jnp.where(side, rb0 - rate * lib, 0.0)
            ib = jnp.where(side, ib0 + rate * lrb, 0.0)
        for row in range(rows):
            to = (row % height) * tx_count + row // height
            out[to, 0, pl.ds(at, 8), :] = re[row]
            out[to, 1, pl.ds(at, 8), :] = im[row]
        return carry

    lax.fori_loop(0, hq // 8, group, 0)


def table_seeds(overall, readings):
    quarter, half = readings // 4, overall // 2
    n = np.stack([2 * np.arange(half) + 1, 2 * np.arange(half) + 2])
    unit = 2 * np.pi / readings
    coarse_t = unit * 8 * np.arange(quarter // 8)[None, :, None] * n[:, None, :]
    fine_t = unit * (np.arange(8) + 0.5)[None, :, None] * n[:, None, :]
    theta = unit * (np.arange(quarter) + 0.5)
    coarse_n = 16 * np.arange(half // 8)[:, None] * theta[None, :]
    fine_n = (2 * np.arange(8)[None, :, None] + np.array([1, 2])[:, None, None]) * theta
    pair = lambda x: np.stack([np.cos(x), np.sin(x)]).astype(np.float32)
    return pair(coarse_t), pair(fine_t), pair(coarse_n), pair(fine_n)


def split(x):
    high = x.astype(jnp.bfloat16)
    return high, (x - high.astype(jnp.float32)).astype(jnp.bfloat16)


def table_kernel(where, coarse_t, fine_t, coarse_n, fine_n, high, low, high_n, low_n):
    del where

    def fill(hi, lo, parity, coarse, fine):
        cos_f, sin_f = fine
        groups = hi.shape[1] // 16

        def step(g, carry):
            cos_rows, sin_rows = [], []
            for j in range(2):
                cos_c, sin_c = coarse(2 * g + j)
                cos_rows.append(cos_c * cos_f - sin_c * sin_f)
                sin_rows.append(sin_c * cos_f + cos_c * sin_f)
            at = pl.ds(pl.multiple_of(g * 16, 16), 16)
            for i, parts in ((0, cos_rows), (1, sin_rows)):
                h, l = split(jnp.concatenate(parts, 0))
                hi[2 * parity + i, at, :] = h
                lo[2 * parity + i, at, :] = l
            return carry

        lax.fori_loop(0, groups, step, 0)

    for parity in range(2):
        fill(
            high,
            low,
            parity,
            lambda g, p=parity: (
                coarse_t[0, p, pl.ds(g, 1), :],
                coarse_t[1, p, pl.ds(g, 1), :],
            ),
            (fine_t[0, parity], fine_t[1, parity]),
        )
        fill(
            high_n,
            low_n,
            parity,
            lambda g: (coarse_n[0, pl.ds(g, 1), :], coarse_n[1, pl.ds(g, 1), :]),
            (fine_n[0, parity], fine_n[1, parity]),
        )


def product(table_high, table_low, x):
    width = x.shape[1]
    high, low = split(x)
    both = jnp.dot(
        table_high, jnp.concatenate([high, low], 1), preferred_element_type=jnp.float32
    )
    rest = jnp.dot(table_low, high, preferred_element_type=jnp.float32)
    return both[:, :width] + (both[:, width:] + rest)


def burgers_kernel(tx_count, readings, where, pixels, high, low, high_n, low_n, *refs):
    *outs, heat, fresh = refs
    h = where[0]
    _, _, hq, breadth = pixels.shape
    harm_count = len(outs)
    half = tx_count // 2
    _, _, count, _ = fresh.shape
    overall = 2 * count

    def gather(c, parity):
        blocks = [
            pixels[g * tx_count + q, c]
            for g in range(harm_count)
            for q in range(parity * half, (parity + 1) * half)
        ]
        return jnp.concatenate(blocks, 0)

    re_odd, re_even = gather(0, 0), gather(0, 1)
    im_odd, im_even = gather(1, 0), gather(1, 1)
    b = product(high[0], low[0], re_odd)
    u = product(high[1], low[1], im_odd)
    a = product(high[2], low[2], re_even)
    v = product(high[3], low[3], im_even)
    scale = 2.0 / (readings * math.sqrt(overall))
    spec_re_odd = (8.0 * scale) * product(high_n[0], low_n[0], a * b + u * v)
    spec_im_odd = (8.0 * scale) * product(high_n[1], low_n[1], a * u + b * v)
    spec_re_even = (4.0 * scale) * product(
        high_n[2], low_n[2], (a * a + b * b) + (u * u + v * v)
    )
    spec_im_even = (8.0 * scale) * product(high_n[3], low_n[3], a * v + b * u)
    index = lax.broadcasted_iota(jnp.int32, (count, breadth), 0)
    total = jnp.zeros((1, breadth), jnp.float32)
    for parity, re, im, s_re, s_im in (
        (0, re_odd, im_odd, spec_re_odd, spec_im_odd),
        (1, re_even, im_even, spec_re_even, spec_im_even),
    ):
        orders = (2 * index + 1 + parity).astype(jnp.float32)
        rate = (nonlinear_gain / overall) * orders
        re_new = re - rate * s_im
        im_new = im + rate * s_re
        total += jnp.sum(orders * (re_new * re_new + im_new * im_new), 0, keepdims=True)
        fresh[0, parity] = re_new
        fresh[1, parity] = im_new
    heat[...] = total
    part = count // harm_count
    for k, out in enumerate(outs):
        at = pl.ds(pl.multiple_of((h ^ k) * part, part), part)
        for c in range(2):
            for parity in range(2):
                out[c, parity] = fresh[c, parity, at, :]


def collect_kernel(where, *refs):
    *blocks, out = refs
    h = where[0]
    height = len(blocks)
    for k, block in enumerate(blocks):
        r = h ^ k
        for c in range(2):
            for parity in range(2):
                at = pl.ds(parity * height + r, block.shape[2], stride=2 * height)
                out[c, at, :] = block[c, parity]


def warm_kernel(ty_count, overall, where, maps, *refs):
    *heats, out, rows_of_heat, field = refs
    h, ty = where[0], where[2]
    height, breadth = out.shape
    lane = lax.broadcasted_iota(jnp.int32, (1, breadth), 1)
    right_side = (lane < breadth // 2) & (ty < ty_count - 1)
    left_side = (lane >= breadth // 2) & (ty > 0)
    side = right_side | left_side
    field[...] = jnp.zeros_like(field)
    rows_of_heat[...] = jnp.zeros_like(rows_of_heat)
    for k, heat in enumerate(heats):
        r = h ^ k
        for part in range(3):
            for tile in range(2):
                rows_of_heat[tile, pl.ds(part * height + r, 1), :] = heat[
                    pl.ds(2 * part + tile, 1), :
                ]
    for part in range(3):
        for tile in range(2):
            for item in range(4):
                field[item, tile, part * height : (part + 1) * height, :] = maps[
                    part, tile, item
                ]
    padded = field.shape[2]

    def tile_of(item, tile):
        value = field[item, tile]
        return value if tile == 0 else jnp.where(side, value, 0.0)

    t, tb = tile_of(0, 0), tile_of(0, 1)
    conduct, conduct_b = tile_of(1, 0), tile_of(1, 1)
    perfuse, perfuse_b = tile_of(2, 0), tile_of(2, 1)
    area = float(overall) * float(overall)
    deposit = tile_of(3, 0) * rows_of_heat[0] / area
    deposit_b = tile_of(3, 1) * jnp.where(side, rows_of_heat[1], 0.0) / area
    for _ in range(4):
        m1, b1 = pltpu.roll(t, breadth - 1, 1), pltpu.roll(tb, breadth - 1, 1)
        m2, b2 = pltpu.roll(t, 1, 1), pltpu.roll(tb, 1, 1)
        m_side = jnp.where(lane == breadth - 1, b1, m1) + jnp.where(lane == 0, b2, m2)
        b_side = jnp.where(lane == breadth - 1, m1, b1) + jnp.where(lane == 0, m2, b2)
        lap = pltpu.roll(t, padded - 1, 0) + pltpu.roll(t, 1, 0) + m_side - 4.0 * t
        lap_b = pltpu.roll(tb, padded - 1, 0) + pltpu.roll(tb, 1, 0) + b_side - 4.0 * tb
        t = t + conduct * lap - perfuse * t + deposit
        tb = tb + conduct_b * lap_b - perfuse_b * tb + deposit_b
    out[...] = t[height : 2 * height]


def beside_ty(tile):
    count = lax.axis_size("ty")
    if count == 2:
        return swap(tile, "ty", 1)
    from_left = lax.ppermute(tile, "ty", [(i, i + 1) for i in range(count - 1)])
    from_right = lax.ppermute(tile, "ty", [(i + 1, i) for i in range(count - 1)])
    lane = lax.broadcasted_iota(jnp.int32, tile.shape, tile.ndim - 1)
    return jnp.where(lane < tile.shape[-1] // 2, from_right, from_left)


def beside_tx(block):
    count = lax.axis_size("tx")
    above = lax.ppermute(block, "tx", [(i, i + 1) for i in range(count - 1)])
    below = lax.ppermute(block, "tx", [(i + 1, i) for i in range(count - 1)])
    return jnp.stack([above, block, below])


def body(
    wave_spectrum,
    lens_window,
    medium_label,
    thermal_excess_prior,
    attenuation_by_kind,
    blood_drain_by_kind,
    diffusivity_by_kind,
):
    _, own, height, breadth = wave_spectrum.shape
    harm_count = lax.axis_size("harm")
    tx_count = lax.axis_size("tx")
    ty_count = lax.axis_size("ty")
    overall = own * harm_count
    assert height == harm_count and 3 * overall < CYCLE_READINGS
    hq = own // tx_count
    rows = height * tx_count
    readings = CYCLE_READINGS
    where = jnp.stack(
        [lax.axis_index("harm"), lax.axis_index("tx"), lax.axis_index("ty")]
    ).astype(jnp.int32)

    blocks = call(
        spread_kernel,
        (where, wave_spectrum.reshape(2, own * height, breadth), lens_window),
        [f32(height, 2, hq, breadth)] * tx_count,
        name="spread",
    )
    blocks = [blocks[0]] + [swap(blocks[k], "tx", k) for k in range(1, tx_count)]

    tiles = -(-rows * STRIP // breadth)
    plane, strips = call(
        strip_kernel,
        (where, *blocks),
        [f32(rows, 2, hq, breadth), f32(tiles, 2, hq, breadth)],
        name="strip",
    )
    if ty_count == 2:
        strips = [swap(strips, "ty", 1)]
    else:
        strips = [
            lax.ppermute(strips, "ty", [(i, i + 1) for i in range(ty_count - 1)]),
            lax.ppermute(strips, "ty", [(i + 1, i) for i in range(ty_count - 1)]),
        ]
    moved = call(
        functools.partial(bend_kernel, tx_count, ty_count, own),
        (where, plane, *strips),
        f32(harm_count * tx_count, 2, hq, breadth),
        name="bend",
    )
    pixels = lax.all_to_all(
        moved.reshape(harm_count * tx_count, 2 * hq, breadth),
        ("harm", "tx"),
        split_axis=0,
        concat_axis=0,
        tiled=True,
    ).reshape(moved.shape)

    quarter = readings // 4
    half = overall // 2
    bf16 = functools.partial(jax.ShapeDtypeStruct, dtype=jnp.bfloat16)
    tables = call(
        table_kernel,
        (where, *(jnp.asarray(s) for s in table_seeds(overall, readings))),
        [bf16((4, quarter, half))] * 2 + [bf16((4, half, quarter))] * 2,
        name="table",
    )

    codes = jnp.arange(attenuation_by_kind.shape[0], dtype=jnp.int32)
    onehot = (medium_label[None, :, :] == codes[:, None, None]).astype(jnp.float32)
    maps = [
        jnp.sum(by_kind[:, None, None] * onehot, axis=0)
        for by_kind in (diffusivity_by_kind, blood_drain_by_kind, attenuation_by_kind)
    ]
    bundle = jnp.stack([thermal_excess_prior, *maps])
    wide = beside_tx(jnp.stack([bundle, beside_ty(bundle)]))

    *fresh, heat = call(
        functools.partial(burgers_kernel, tx_count, readings),
        (where, pixels, *tables),
        [f32(2, 2, own // 2, breadth)] * harm_count + [f32(1, breadth)],
        scratch=[pltpu.VMEM((2, 2, half, breadth), jnp.float32)],
        name="burgers",
    )
    fresh = [fresh[0]] + [swap(fresh[k], "harm", k) for k in range(1, harm_count)]
    heat = jnp.concatenate([heat, beside_ty(heat)])
    heat = beside_tx(heat).reshape(6, breadth)
    heats = [heat] + [swap(heat, "harm", k) for k in range(1, harm_count)]
    padded = -(-3 * height // 8) * 8
    later = call(
        functools.partial(warm_kernel, ty_count, overall),
        (where, wide, *heats),
        f32(height, breadth),
        scratch=[
            pltpu.VMEM((2, padded, breadth), jnp.float32),
            pltpu.VMEM((4, 2, padded, breadth), jnp.float32),
        ],
        name="warm",
    )
    field = call(
        collect_kernel,
        (where, *fresh),
        f32(2, own * height, breadth),
        name="collect",
    )
    return field.reshape(2, own, height, breadth), later


def solution(mesh):
    in_specs = (
        P(None, "harm", "tx", "ty"),
        P("tx", "ty"),
        P("tx", "ty"),
        P("tx", "ty"),
        P(),
        P(),
        P(),
    )
    out_specs = (P(None, "harm", "tx", "ty"), P("tx", "ty"))
    return jax.shard_map(body, mesh=mesh, in_specs=in_specs, out_specs=out_specs, check_vma=False)
```

```python
import functools
import math

import jax
import jax.numpy as jnp
import numpy as np
from jax import lax
from jax.experimental import pallas as pl
from jax.experimental.pallas import tpu as pltpu
from jax.sharding import PartitionSpec as P

CYCLE_READINGS = 2048
diffraction_gain = 0.3
nonlinear_gain = 0.3
ORDER = 4
STRIP = 2 * ORDER
GRANT = 16 * 2**20

VMEM = pl.BlockSpec(memory_space=pltpu.VMEM)
SMEM = pl.BlockSpec(memory_space=pltpu.SMEM)
HBM = pl.BlockSpec(memory_space=pltpu.HBM)


def call(kernel, args, outs, scratch=(), steps=1, places=None, out_specs=None):
    places = places or [VMEM] * len(args)
    spaces = {id(VMEM): pltpu.VMEM, id(HBM): pltpu.HBM}
    args = [
        pltpu.with_memory_space_constraint(a, spaces[id(place)]) if id(place) in spaces else a
        for a, place in zip(args, places)
    ]
    if out_specs is None:
        out_specs = jax.tree.map(lambda _: VMEM, outs)
        outs = jax.tree.map(lambda o: pltpu.VMEM(o.shape, o.dtype), outs)
    return pl.pallas_call(
        kernel,
        grid=(steps,),
        out_shape=outs,
        in_specs=places,
        out_specs=out_specs,
        scratch_shapes=scratch,
        compiler_params=pltpu.CompilerParams(vmem_limit_bytes=GRANT),
    )(*args)


def f32(*shape):
    return jax.ShapeDtypeStruct(shape, jnp.float32)


def swap(block, axis, k):
    count = lax.axis_size(axis)
    return lax.ppermute(block, axis, [(i, i ^ k) for i in range(count)])


def first_harmonic(h, q, own, hq, half):
    return h * own + 1 + q // half + 2 * lax.rem(q, half) * hq


def spread_kernel(where, wave, lens, *refs):
    *outs, tile, window, sems = refs
    copies = [
        pltpu.make_async_copy(lens, window, sems.at[0]),
        pltpu.make_async_copy(wave.at[0], tile.at[0], sems.at[1]),
        pltpu.make_async_copy(wave.at[1], tile.at[1], sems.at[2]),
    ]
    for copy in copies:
        copy.start()
    tx = where[1]
    half = len(outs) // 2
    height, _, hq, _ = outs[0].shape
    copies[0].wait()
    weight = 0.25 + 0.75 * window[...].astype(jnp.float32)
    for c in range(2):
        copies[1 + c].wait()
        for k, out in enumerate(outs):
            q = tx ^ k
            start = (q // half + 2 * lax.rem(q, half) * hq) * height
            for r in range(height):
                rows = tile[c, pl.ds(start + r, hq, stride=2 * height), :]
                out[r, c] = rows * weight[r : r + 1, :]


def look_kernel(conduct, perfuse, absorb, label, prior, bundle):
    bundle[0] = prior[...]
    kinds = label[...]
    for item, table in ((1, conduct), (2, perfuse), (3, absorb)):
        values = jnp.zeros(kinds.shape, jnp.float32)
        for kind in range(table.shape[0]):
            values = jnp.where(kinds == kind, table[kind], values)
        bundle[item] = values


def strip_kernel(where, *refs):
    *blocks, plane, strips = refs
    tx = where[1]
    height, _, hq, _ = blocks[0].shape
    rows, _, _, breadth = plane.shape
    for k, block in enumerate(blocks):
        base = (tx ^ k) * height
        for r in range(height):
            plane[base + r] = block[r]
    per = breadth // STRIP
    lane = lax.broadcasted_iota(jnp.int32, (hq, breadth), 1) // STRIP
    for t in range(strips.shape[0]):
        for c in range(2):
            packed = jnp.zeros((hq, breadth), jnp.float32)
            for i in range(min(per, rows - t * per)):
                rolled = pltpu.roll(plane[t * per + i, c], STRIP * i + ORDER, 1)
                packed = jnp.where(lane == i, rolled, packed)
            strips[t, c] = packed


def column_powers(breadth, ty_count):
    kinds = {1: [(1, 1)], 2: [(1, 0), (0, 1)]}.get(ty_count, [(1, 0), (0, 0), (0, 1)])
    wide = breadth + STRIP
    out = []
    for at_left, at_right in kinds:
        step = np.eye(wide, k=1) + np.eye(wide, k=-1) - 2 * np.eye(wide)
        outside = np.zeros(wide, bool)
        outside[:ORDER] = at_left
        outside[wide - ORDER :] = at_right
        step[outside] = 0
        step[:, outside] = 0
        power, powers = np.eye(wide), []
        for _ in range(ORDER):
            power = power @ step
            powers.append(power[:, ORDER : ORDER + breadth])
        powers = np.concatenate(powers, 1)
        past = np.concatenate([powers[:ORDER], powers[wide - ORDER :]])
        out.append(np.concatenate([powers[ORDER : ORDER + breadth], np.tile(past, (breadth // STRIP, 1))]))
    return np.stack(out)


def bend_kernel(tx_count, ty_count, own, where, plane, powers, *refs):
    *strips, out, shifted = refs
    h, tx, ty = where[0], where[1], where[2]
    rows, _, hq, breadth = plane.shape
    height = rows // tx_count
    per = breadth // STRIP
    lane = lax.broadcasted_iota(jnp.int32, (hq, breadth), 1)
    matrix = powers[
        jnp.where(ty == 0, 0, jnp.where(ty == ty_count - 1, powers.shape[0] - 1, 1))
    ]
    along, past = matrix[:breadth], matrix[breadth:]
    right = jnp.concatenate([along, along, past, past], 0)
    for c in range(2):
        packs = []
        for t in range(strips[0].shape[0]):
            piece = strips[0][t, c]
            if len(strips) == 2:
                piece = jnp.where(lane % STRIP < ORDER, piece, strips[1][t, c])
            packs.append(piece)
        inside = [plane[row, c] for row in range(rows)]
        beyond = [
            jnp.where(lane // STRIP == row % per, packs[row // per], 0.0)
            for row in range(rows)
        ]
        left = split(jnp.concatenate(inside, 0)) + split(jnp.concatenate(beyond, 0))
        shifted[c] = jnp.dot(
            jnp.concatenate(left, 1), right, preferred_element_type=jnp.float32
        )
    low = first_harmonic(h, tx, own, hq, tx_count // 2)
    inner = lax.broadcasted_iota(jnp.int32, (8, breadth), 0)
    zero = jnp.zeros((8, breadth), jnp.float32)

    def across(v):
        return [
            ((v[row + 1] if row < rows - 1 else zero) + (v[row - 1] if row else zero))
            - 2.0 * v[row]
            for row in range(rows)
        ]

    def group(g, carry):
        at = pl.multiple_of(g * 8, 8)
        gain = diffraction_gain / (low + 2 * (at + inner)).astype(jnp.float32)

        def power(c, b):
            return [
                shifted[c, pl.ds(row * hq + at, 8), (b - 1) * breadth : b * breadth]
                for row in range(rows)
            ]

        base = [[plane[row, c, pl.ds(at, 8), :] for row in range(rows)] for c in range(2)]
        re, im = base
        factor = gain
        for b, divider in ((1, 4.0), (2, 3.0), (3, 2.0), (4, 1.0)):
            p_re, p_im = power(0, b), power(1, b)
            if b % 4 == 1:
                p_re, p_im, signs = p_im, p_re, (-1.0, 1.0)
            elif b % 4 == 2:
                signs = (-1.0, -1.0)
            elif b % 4 == 3:
                p_re, p_im, signs = p_im, p_re, (1.0, -1.0)
            else:
                signs = (1.0, 1.0)
            base = [
                [v + (signs[c] * factor) * p for v, p in zip(base[c], (p_re, p_im)[c])]
                for c in range(2)
            ]
            factor = factor * gain * (1.0 / (b + 1))
            rate = gain * (1.0 / divider)
            lap_re, lap_im = across(re), across(im)
            re = [v - rate * l for v, l in zip(base[0], lap_im)]
            im = [v + rate * l for v, l in zip(base[1], lap_re)]
        for row in range(rows):
            to = (row % height) * tx_count + row // height
            out[to, 0, pl.ds(at, 8), :] = re[row]
            out[to, 1, pl.ds(at, 8), :] = im[row]
        return carry

    lax.fori_loop(0, hq // 8, group, 0)


def table_seeds(overall):
    half = overall // 2
    unit = np.pi / (2 * overall)
    even = 2 * np.arange(half) + 2
    rows, eight = np.arange(half // 8)[:, None], np.arange(8)[:, None]
    theta = unit * (np.arange(half) + 0.5)
    coarse = [16 * rows * theta, 8 * rows * unit * even, 16 * rows * theta]
    fine = [(2 * eight + 1) * theta, unit * (eight + 0.5) * even, (2 * eight + 2) * theta]
    pair = lambda x: np.stack([np.cos(x), np.sin(x)], 1).astype(np.float32)
    return pair(np.stack(coarse)), pair(np.stack(fine))


def split(x):
    high = x.astype(jnp.bfloat16)
    return high, (x - high.astype(jnp.float32)).astype(jnp.bfloat16)


def table_kernel(coarse, fine, high, low):
    for kind in range(coarse.shape[0]):
        cos_f, sin_f = fine[kind, 0], fine[kind, 1]

        def step(g, carry, kind=kind, cos_f=cos_f, sin_f=sin_f):
            cos_rows, sin_rows = [], []
            for j in range(2):
                cos_c = coarse[kind, 0, pl.ds(2 * g + j, 1), :]
                sin_c = coarse[kind, 1, pl.ds(2 * g + j, 1), :]
                cos_rows.append(cos_c * cos_f - sin_c * sin_f)
                sin_rows.append(sin_c * cos_f + cos_c * sin_f)
            at = pl.ds(pl.multiple_of(g * 16, 16), 16)
            for i, parts in enumerate((cos_rows, sin_rows)):
                h, l = split(jnp.concatenate(parts, 0))
                high[kind, i, at, :] = h
                low[kind, i, at, :] = l
            return carry

        lax.fori_loop(0, high.shape[2] // 16, step, 0)


def product(high, low, kind, i, *columns):
    width = columns[0].shape[1]
    parts = [split(x) for x in columns]
    full = jnp.dot(
        high[kind, i],
        jnp.concatenate([p for pair in parts for p in pair], 1),
        preferred_element_type=jnp.float32,
    )
    rest = jnp.dot(
        low[kind, i],
        jnp.concatenate([pair[0] for pair in parts], 1),
        preferred_element_type=jnp.float32,
    )
    return [
        full[:, 2 * j * width : (2 * j + 1) * width]
        + (
            full[:, (2 * j + 1) * width : (2 * j + 2) * width]
            + rest[:, j * width : (j + 1) * width]
        )
        for j in range(len(columns))
    ]


def burgers_kernel(tx_count, where, pixels, high, low, *refs):
    *outs, heat, fresh = refs
    h = where[0]
    _, _, _, breadth = pixels.shape
    harm_count = len(outs)
    half = tx_count // 2
    count = fresh.shape[2]
    overall = 2 * count
    ODD, BY_TIME, BY_ORDER = 0, 1, 2

    def gather(c, parity):
        blocks = [
            pixels[g * tx_count + q, c]
            for g in range(harm_count)
            for q in range(parity * half, (parity + 1) * half)
        ]
        return jnp.concatenate(blocks, 0)

    index = lax.broadcasted_iota(jnp.int32, (count, breadth), 0)
    flip = jnp.where(index % 2 == 0, 1.0, -1.0)
    re_odd, re_even = gather(0, 0), gather(0, 1)
    im_odd, im_even = gather(1, 0), gather(1, 1)
    b0, u1 = product(high, low, ODD, 0, re_odd, flip * im_odd)
    u0, b1 = product(high, low, ODD, 1, im_odd, flip * re_odd)
    a0, a1 = product(high, low, BY_TIME, 0, re_even, -flip * re_even)
    v0, v1 = product(high, low, BY_TIME, 1, im_even, flip * im_even)
    scale = 1.0 / (2 * overall * math.sqrt(overall))
    cos0, sin0 = product(high, low, ODD, 0, a0 * b0 + u0 * v0, a1 * u1 + b1 * v1)
    sin1, cos1 = product(high, low, ODD, 1, a0 * u0 + b0 * v0, a1 * b1 + u1 * v1)
    spec_re_odd = (8.0 * scale) * (cos0 + flip * cos1)
    spec_im_odd = (8.0 * scale) * (sin1 + flip * sin0)
    even0, even1 = product(
        high,
        low,
        BY_ORDER,
        0,
        (a0 * a0 + b0 * b0) + (u0 * u0 + v0 * v0),
        (a1 * a1 + b1 * b1) + (u1 * u1 + v1 * v1),
    )
    spec_re_even = (4.0 * scale) * (even0 - flip * even1)
    even0, even1 = product(
        high, low, BY_ORDER, 1, a0 * v0 + b0 * u0, a1 * v1 + b1 * u1
    )
    spec_im_even = (8.0 * scale) * (even0 + flip * even1)
    total = jnp.zeros((1, breadth), jnp.float32)
    for parity, re, im, s_re, s_im in (
        (0, re_odd, im_odd, spec_re_odd, spec_im_odd),
        (1, re_even, im_even, spec_re_even, spec_im_even),
    ):
        orders = (2 * index + 1 + parity).astype(jnp.float32)
        rate = (nonlinear_gain / overall) * orders
        re_new = re - rate * s_im
        im_new = im + rate * s_re
        total += jnp.sum(orders * (re_new * re_new + im_new * im_new), 0, keepdims=True)
        fresh[0, parity] = re_new
        fresh[1, parity] = im_new
    heat[...] = jnp.broadcast_to(total[None], heat.shape)
    part = count // harm_count
    for k, out in enumerate(outs):
        at = pl.ds(pl.multiple_of((h ^ k) * part, part), part)
        for c in range(2):
            for parity in range(2):
                out[c, parity] = fresh[c, parity, at, :]


def collect_kernel(parts, where, *refs):
    *blocks, out = refs
    h = where[0]
    height = len(blocks)
    c, part = pl.program_id(0) // parts, lax.rem(pl.program_id(0), parts)
    count = blocks[0].shape[2] // parts
    for k, block in enumerate(blocks):
        r = h ^ k
        for parity in range(2):
            at = pl.ds(parity * height + r, count, stride=2 * height)
            out[0, at, :] = block[c, parity, pl.ds(pl.multiple_of(part * count, count), count), :]


def join_kernel(own, other, out):
    out[0] = own[...]
    out[1] = other[...]


def warm_kernel(tx_count, ty_count, overall, where, above, level, below, heats, *refs):
    out, rows_of_heat, field = refs
    maps = (above, level, below)
    tx, ty = where[1], where[2]
    height, breadth = out.shape
    lane = lax.broadcasted_iota(jnp.int32, (1, breadth), 1)
    right_side = (lane < breadth // 2) & (ty < ty_count - 1)
    left_side = (lane >= breadth // 2) & (ty > 0)
    side = right_side | left_side
    field[...] = jnp.zeros_like(field)
    rows_of_heat[...] = jnp.zeros_like(rows_of_heat)
    for part in range(3):
        tile_row = jnp.clip(tx + part - 1, 0, tx_count - 1)
        for r in range(height):
            at = (r * tx_count + tile_row) * ty_count
            left = heats[at + jnp.maximum(ty - 1, 0)]
            right = heats[at + jnp.minimum(ty + 1, ty_count - 1)]
            to = slice(part * height + r, part * height + r + 1)
            rows_of_heat[0, to, :] = heats[at + ty]
            rows_of_heat[1, to, :] = jnp.where(lane < breadth // 2, right, left)
    for part in range(3):
        for tile in range(2):
            for item in range(4):
                field[item, tile, part * height : (part + 1) * height, :] = maps[
                    part
                ][tile, item]
    padded = field.shape[2]

    def tile_of(item, tile):
        value = field[item, tile]
        return value if tile == 0 else jnp.where(side, value, 0.0)

    t, tb = tile_of(0, 0), tile_of(0, 1)
    conduct, conduct_b = tile_of(1, 0), tile_of(1, 1)
    perfuse, perfuse_b = tile_of(2, 0), tile_of(2, 1)
    area = float(overall) * float(overall)
    deposit = tile_of(3, 0) * rows_of_heat[0] / area
    deposit_b = tile_of(3, 1) * jnp.where(side, rows_of_heat[1], 0.0) / area
    for _ in range(4):
        m1, b1 = pltpu.roll(t, breadth - 1, 1), pltpu.roll(tb, breadth - 1, 1)
        m2, b2 = pltpu.roll(t, 1, 1), pltpu.roll(tb, 1, 1)
        m_side = jnp.where(lane == breadth - 1, b1, m1) + jnp.where(lane == 0, b2, m2)
        b_side = jnp.where(lane == breadth - 1, m1, b1) + jnp.where(lane == 0, m2, b2)
        lap = pltpu.roll(t, padded - 1, 0) + pltpu.roll(t, 1, 0) + m_side - 4.0 * t
        lap_b = pltpu.roll(tb, padded - 1, 0) + pltpu.roll(tb, 1, 0) + b_side - 4.0 * tb
        t = t + conduct * lap - perfuse * t + deposit
        tb = tb + conduct_b * lap_b - perfuse_b * tb + deposit_b
    out[...] = t[height : 2 * height]


def beside_ty(tile):
    count = lax.axis_size("ty")
    if count == 2:
        return swap(tile, "ty", 1)
    from_left = lax.ppermute(tile, "ty", [(i, i + 1) for i in range(count - 1)])
    from_right = lax.ppermute(tile, "ty", [(i + 1, i) for i in range(count - 1)])
    lane = lax.broadcasted_iota(jnp.int32, tile.shape, tile.ndim - 1)
    return jnp.where(lane < tile.shape[-1] // 2, from_right, from_left)


def beside_tx(block):
    count = lax.axis_size("tx")
    above = lax.ppermute(block, "tx", [(i, i + 1) for i in range(count - 1)])
    below = lax.ppermute(block, "tx", [(i + 1, i) for i in range(count - 1)])
    return above, block, below


def body(
    wave_spectrum,
    lens_window,
    medium_label,
    thermal_excess_prior,
    attenuation_by_kind,
    blood_drain_by_kind,
    diffusivity_by_kind,
):
    _, own, height, breadth = wave_spectrum.shape
    harm_count = lax.axis_size("harm")
    tx_count = lax.axis_size("tx")
    ty_count = lax.axis_size("ty")
    overall = own * harm_count
    assert height == harm_count and CYCLE_READINGS == 4 * overall
    hq = own // tx_count
    rows = height * tx_count
    where = jnp.stack(
        [lax.axis_index("harm"), lax.axis_index("tx"), lax.axis_index("ty")]
    ).astype(jnp.int32)

    small = (height, breadth)
    blocks = call(
        spread_kernel,
        (where, wave_spectrum.reshape(2, own * height, breadth), lens_window),
        [f32(height, 2, hq, breadth)] * tx_count,
        scratch=[
            pltpu.VMEM((2, own * height, breadth), jnp.float32),
            pltpu.VMEM(small, jnp.int32),
            pltpu.SemaphoreType.DMA((3,)),
        ],
        places=[SMEM, HBM, HBM],
    )
    blocks = [blocks[0]] + [swap(blocks[k], "tx", k) for k in range(1, tx_count)]

    tiles = -(-rows * STRIP // breadth)
    plane, strips = call(
        strip_kernel,
        (where, *blocks),
        [f32(rows, 2, hq, breadth), f32(tiles, 2, hq, breadth)],
        places=[SMEM] + [VMEM] * tx_count,
    )
    if ty_count == 2:
        strips = [swap(strips, "ty", 1)]
    else:
        strips = [
            lax.ppermute(strips, "ty", [(i, i + 1) for i in range(ty_count - 1)]),
            lax.ppermute(strips, "ty", [(i + 1, i) for i in range(ty_count - 1)]),
        ]
    owners = harm_count * tx_count
    moved = call(
        functools.partial(bend_kernel, tx_count, ty_count, own),
        (
            where,
            plane,
            jnp.asarray(column_powers(breadth, ty_count), jnp.bfloat16),
            *strips,
        ),
        f32(owners, 2, hq, breadth),
        scratch=[pltpu.VMEM((2, rows * hq, ORDER * breadth), jnp.float32)],
        places=[SMEM] + [VMEM] * (2 + len(strips)),
        out_specs=VMEM,
    )
    moved, medium_label = lax.optimization_barrier((moved, medium_label))
    pixels = lax.all_to_all(
        moved.reshape(owners, 2 * hq, breadth),
        ("harm", "tx"),
        split_axis=0,
        concat_axis=0,
        tiled=True,
    ).reshape(moved.shape)

    half = overall // 2
    coarse, fine = (jnp.asarray(x) for x in table_seeds(overall))
    table = jax.ShapeDtypeStruct((3, 2, half, half), jnp.bfloat16)
    tables = call(table_kernel, (coarse, fine), [table] * 2)
    bundle = call(
        look_kernel,
        (
            diffusivity_by_kind,
            blood_drain_by_kind,
            attenuation_by_kind,
            medium_label,
            thermal_excess_prior,
        ),
        f32(4, *small),
        places=[SMEM] * 3 + [VMEM] * 2,
    )
    wide = call(join_kernel, (bundle, beside_ty(bundle)), f32(2, *bundle.shape))
    maps = beside_tx(wide)
    pixels, maps = lax.optimization_barrier((pixels, maps))

    *fresh, heat = call(
        functools.partial(burgers_kernel, tx_count),
        (where, pixels, *tables),
        [f32(2, 2, own // 2, breadth)] * harm_count + [f32(owners * ty_count, 1, breadth)],
        scratch=[pltpu.VMEM((2, 2, half, breadth), jnp.float32)],
        places=[SMEM] + [VMEM] * 3,
    )
    fresh = [fresh[0]] + [swap(fresh[k], "harm", k) for k in range(1, harm_count)]
    heats = lax.all_to_all(
        heat, ("harm", "tx", "ty"), split_axis=0, concat_axis=0, tiled=True
    )
    padded = -(-3 * height // 8) * 8
    later = call(
        functools.partial(warm_kernel, tx_count, ty_count, overall),
        (where, *maps, heats),
        f32(*small),
        scratch=[
            pltpu.VMEM((2, padded, breadth), jnp.float32),
            pltpu.VMEM((4, 2, padded, breadth), jnp.float32),
        ],
        places=[SMEM] + [VMEM] * 4,
        out_specs=VMEM,
    )
    parts = 2
    field = call(
        functools.partial(collect_kernel, parts),
        (where, *fresh),
        f32(2, own * height, breadth),
        steps=2 * parts,
        places=[SMEM] + [VMEM] * harm_count,
        out_specs=pl.BlockSpec(
            (1, own * height // parts, breadth), lambda g: (g // parts, g % parts, 0)
        ),
    )
    return field.reshape(2, own, height, breadth), later


def solution(mesh):
    in_specs = (
        P(None, "harm", "tx", "ty"),
        P("tx", "ty"),
        P("tx", "ty"),
        P("tx", "ty"),
        P(),
        P(),
        P(),
    )
    out_specs = (P(None, "harm", "tx", "ty"), P("tx", "ty"))
    return jax.shard_map(body, mesh=mesh, in_specs=in_specs, out_specs=out_specs, check_vma=False)
```

```python
import functools
import math

import jax
import jax.numpy as jnp
import numpy as np
from jax import lax
from jax.experimental import pallas as pl
from jax.experimental.pallas import tpu as pltpu
from jax.sharding import PartitionSpec as P

CYCLE_READINGS = 2048
diffraction_gain = 0.3
nonlinear_gain = 0.3
ORDER = 4
STRIP = 2 * ORDER
GRANT = 16 * 2**20

VMEM = pl.BlockSpec(memory_space=pltpu.VMEM)
SMEM = pl.BlockSpec(memory_space=pltpu.SMEM)
HBM = pl.BlockSpec(memory_space=pltpu.HBM)


def call(kernel, args, outs, scratch=(), places=None, out_specs=None):
    places = places or [VMEM] * len(args)
    spaces = {id(VMEM): pltpu.VMEM, id(HBM): pltpu.HBM}
    args = [
        pltpu.with_memory_space_constraint(a, spaces[id(place)]) if id(place) in spaces else a
        for a, place in zip(args, places)
    ]
    if out_specs is None:
        out_specs = jax.tree.map(lambda _: VMEM, outs)
        outs = jax.tree.map(lambda o: pltpu.VMEM(o.shape, o.dtype), outs)
    return pl.pallas_call(
        kernel,
        out_shape=outs,
        in_specs=places,
        out_specs=out_specs,
        scratch_shapes=scratch,
        compiler_params=pltpu.CompilerParams(vmem_limit_bytes=GRANT),
    )(*args)


def f32(*shape):
    return jax.ShapeDtypeStruct(shape, jnp.float32)


def swap(block, axis, k):
    count = lax.axis_size(axis)
    return lax.ppermute(block, axis, [(i, i ^ k) for i in range(count)])


def first_harmonic(h, q, own, hq, half):
    return h * own + 1 + q // half + 2 * lax.rem(q, half) * hq


def spread_kernel(where, wave, lens, *refs):
    *outs, tile, window, sems = refs
    copies = [
        pltpu.make_async_copy(lens, window, sems.at[0]),
        pltpu.make_async_copy(wave.at[0], tile.at[0], sems.at[1]),
        pltpu.make_async_copy(wave.at[1], tile.at[1], sems.at[2]),
    ]
    for copy in copies:
        copy.start()
    tx = where[1]
    half = len(outs) // 2
    height, _, hq, _ = outs[0].shape
    copies[0].wait()
    weight = 0.25 + 0.75 * window[...].astype(jnp.float32)
    for c in range(2):
        copies[1 + c].wait()
        for k, out in enumerate(outs):
            q = tx ^ k
            start = (q // half + 2 * lax.rem(q, half) * hq) * height
            for r in range(height):
                rows = tile[c, pl.ds(start + r, hq, stride=2 * height), :]
                out[r, c] = rows * weight[r : r + 1, :]


def strip_kernel(where, *refs):
    *blocks, plane, strips = refs
    tx = where[1]
    height, _, hq, _ = blocks[0].shape
    rows, _, _, breadth = plane.shape
    for k, block in enumerate(blocks):
        base = (tx ^ k) * height
        for r in range(height):
            plane[base + r] = block[r]
    per = breadth // STRIP
    lane = lax.broadcasted_iota(jnp.int32, (hq, breadth), 1) // STRIP
    for t in range(strips.shape[0]):
        for c in range(2):
            packed = jnp.zeros((hq, breadth), jnp.float32)
            for i in range(min(per, rows - t * per)):
                rolled = pltpu.roll(plane[t * per + i, c], STRIP * i + ORDER, 1)
                packed = jnp.where(lane == i, rolled, packed)
            strips[t, c] = packed


def column_powers(breadth, ty_count):
    kinds = {1: [(1, 1)], 2: [(1, 0), (0, 1)]}.get(ty_count, [(1, 0), (0, 0), (0, 1)])
    wide = breadth + STRIP
    out = []
    for at_left, at_right in kinds:
        step = np.eye(wide, k=1) + np.eye(wide, k=-1) - 2 * np.eye(wide)
        outside = np.zeros(wide, bool)
        outside[:ORDER] = at_left
        outside[wide - ORDER :] = at_right
        step[outside] = 0
        step[:, outside] = 0
        power, powers = np.eye(wide), []
        for _ in range(ORDER):
            power = power @ step
            powers.append(power[:, ORDER : ORDER + breadth])
        powers = np.concatenate(powers, 1)
        past = np.concatenate([powers[:ORDER], powers[wide - ORDER :]])
        out.append(np.concatenate([powers[ORDER : ORDER + breadth], np.tile(past, (breadth // STRIP, 1))]))
    return np.stack(out)


def bend_kernel(tx_count, ty_count, own, where, plane, powers, *refs):
    *strips, out, shifted, stage, sems = refs
    h, tx, ty = where[0], where[1], where[2]
    rows, _, hq, breadth = plane.shape
    height = rows // tx_count
    per = breadth // STRIP
    lane = lax.broadcasted_iota(jnp.int32, (hq, breadth), 1)
    matrix = powers[
        jnp.where(ty == 0, 0, jnp.where(ty == ty_count - 1, powers.shape[0] - 1, 1))
    ]
    along, past = matrix[:breadth], matrix[breadth:]
    right = jnp.concatenate([along, along, past, past], 0)
    for c in range(2):
        packs = []
        for t in range(strips[0].shape[0]):
            piece = strips[0][t, c]
            if len(strips) == 2:
                piece = jnp.where(lane % STRIP < ORDER, piece, strips[1][t, c])
            packs.append(piece)
        inside = [plane[row, c] for row in range(rows)]
        beyond = [
            jnp.where(lane // STRIP == row % per, packs[row // per], 0.0)
            for row in range(rows)
        ]
        left = split(jnp.concatenate(inside, 0)) + split(jnp.concatenate(beyond, 0))
        shifted[c] = jnp.dot(
            jnp.concatenate(left, 1), right, preferred_element_type=jnp.float32
        )
    low = first_harmonic(h, tx, own, hq, tx_count // 2)
    inner = lax.broadcasted_iota(jnp.int32, (8, breadth), 0)
    zero = jnp.zeros((8, breadth), jnp.float32)

    def across(v):
        return [
            ((v[row + 1] if row < rows - 1 else zero) + (v[row - 1] if row else zero))
            - 2.0 * v[row]
            for row in range(rows)
        ]

    def group(g, carry):
        at = pl.multiple_of(g * 8, 8)
        gain = diffraction_gain / (low + 2 * (at + inner)).astype(jnp.float32)

        def power(c, b):
            return [
                shifted[c, pl.ds(row * hq + at, 8), (b - 1) * breadth : b * breadth]
                for row in range(rows)
            ]

        base = [[plane[row, c, pl.ds(at, 8), :] for row in range(rows)] for c in range(2)]
        re, im = base
        factor = gain
        for b, divider in ((1, 4.0), (2, 3.0), (3, 2.0), (4, 1.0)):
            p_re, p_im = power(0, b), power(1, b)
            if b % 4 == 1:
                p_re, p_im, signs = p_im, p_re, (-1.0, 1.0)
            elif b % 4 == 2:
                signs = (-1.0, -1.0)
            elif b % 4 == 3:
                p_re, p_im, signs = p_im, p_re, (1.0, -1.0)
            else:
                signs = (1.0, 1.0)
            base = [
                [v + (signs[c] * factor) * p for v, p in zip(base[c], (p_re, p_im)[c])]
                for c in range(2)
            ]
            factor = factor * gain * (1.0 / (b + 1))
            rate = gain * (1.0 / divider)
            lap_re, lap_im = across(re), across(im)
            re = [v - rate * l for v, l in zip(base[0], lap_im)]
            im = [v + rate * l for v, l in zip(base[1], lap_re)]
        for row in range(rows):
            to = (row % height) * tx_count + row // height
            stage[g, to, 0] = re[row]
            stage[g, to, 1] = im[row]
        write(g).start()
        return carry

    def write(g):
        at = pl.ds(pl.multiple_of(g * 8, 8), 8)
        return pltpu.make_async_copy(stage.at[g], out.at[:, :, at, :], sems.at[g])

    lax.fori_loop(0, hq // 8, group, 0)
    for g in range(hq // 8):
        write(g).wait()


def table_seeds(overall):
    half = overall // 2
    unit = np.pi / (2 * overall)
    even = 2 * np.arange(half) + 2
    rows, eight = np.arange(half // 8)[:, None], np.arange(8)[:, None]
    theta = unit * (np.arange(half) + 0.5)
    coarse = [16 * rows * theta, 8 * rows * unit * even, 16 * rows * theta]
    fine = [(2 * eight + 1) * theta, unit * (eight + 0.5) * even, (2 * eight + 2) * theta]
    pair = lambda x: np.stack([np.cos(x), np.sin(x)], 1).astype(np.float32)
    return pair(np.stack(coarse)), pair(np.stack(fine))


def split(x):
    high = x.astype(jnp.bfloat16)
    return high, (x - high.astype(jnp.float32)).astype(jnp.bfloat16)


def table_kernel(coarse, fine, high, low):
    for kind in range(coarse.shape[0]):
        cos_f, sin_f = fine[kind, 0], fine[kind, 1]

        def step(g, carry, kind=kind, cos_f=cos_f, sin_f=sin_f):
            cos_rows, sin_rows = [], []
            for j in range(2):
                cos_c = coarse[kind, 0, pl.ds(2 * g + j, 1), :]
                sin_c = coarse[kind, 1, pl.ds(2 * g + j, 1), :]
                cos_rows.append(cos_c * cos_f - sin_c * sin_f)
                sin_rows.append(sin_c * cos_f + cos_c * sin_f)
            at = pl.ds(pl.multiple_of(g * 16, 16), 16)
            for i, parts in enumerate((cos_rows, sin_rows)):
                h, l = split(jnp.concatenate(parts, 0))
                high[kind, i, at, :] = h
                low[kind, i, at, :] = l
            return carry

        lax.fori_loop(0, high.shape[2] // 16, step, 0)


def product(high, low, kind, i, *columns):
    width = columns[0].shape[1]
    parts = [split(x) for x in columns]
    full = jnp.dot(
        high[kind, i],
        jnp.concatenate([p for pair in parts for p in pair], 1),
        preferred_element_type=jnp.float32,
    )
    rest = jnp.dot(
        low[kind, i],
        jnp.concatenate([pair[0] for pair in parts], 1),
        preferred_element_type=jnp.float32,
    )
    return [
        full[:, 2 * j * width : (2 * j + 1) * width]
        + (
            full[:, (2 * j + 1) * width : (2 * j + 2) * width]
            + rest[:, j * width : (j + 1) * width]
        )
        for j in range(len(columns))
    ]


def burgers_kernel(tx_count, where, pixels, high, low, *refs):
    *outs, heat, fresh = refs
    h = where[0]
    _, _, _, breadth = pixels.shape
    harm_count = len(outs)
    half = tx_count // 2
    count = fresh.shape[2]
    overall = 2 * count
    ODD, BY_TIME, BY_ORDER = 0, 1, 2

    def gather(c, parity):
        blocks = [
            pixels[g * tx_count + q, c]
            for g in range(harm_count)
            for q in range(parity * half, (parity + 1) * half)
        ]
        return jnp.concatenate(blocks, 0)

    index = lax.broadcasted_iota(jnp.int32, (count, breadth), 0)
    flip = jnp.where(index % 2 == 0, 1.0, -1.0)
    re_odd, re_even = gather(0, 0), gather(0, 1)
    im_odd, im_even = gather(1, 0), gather(1, 1)
    b0, u1 = product(high, low, ODD, 0, re_odd, flip * im_odd)
    u0, b1 = product(high, low, ODD, 1, im_odd, flip * re_odd)
    a0, a1 = product(high, low, BY_TIME, 0, re_even, -flip * re_even)
    v0, v1 = product(high, low, BY_TIME, 1, im_even, flip * im_even)
    scale = 1.0 / (2 * overall * math.sqrt(overall))
    cos0, sin0 = product(high, low, ODD, 0, a0 * b0 + u0 * v0, a1 * u1 + b1 * v1)
    sin1, cos1 = product(high, low, ODD, 1, a0 * u0 + b0 * v0, a1 * b1 + u1 * v1)
    spec_re_odd = (8.0 * scale) * (cos0 + flip * cos1)
    spec_im_odd = (8.0 * scale) * (sin1 + flip * sin0)
    even0, even1 = product(
        high,
        low,
        BY_ORDER,
        0,
        (a0 * a0 + b0 * b0) + (u0 * u0 + v0 * v0),
        (a1 * a1 + b1 * b1) + (u1 * u1 + v1 * v1),
    )
    spec_re_even = (4.0 * scale) * (even0 - flip * even1)
    even0, even1 = product(
        high, low, BY_ORDER, 1, a0 * v0 + b0 * u0, a1 * v1 + b1 * u1
    )
    spec_im_even = (8.0 * scale) * (even0 + flip * even1)
    total = jnp.zeros((1, breadth), jnp.float32)
    for parity, re, im, s_re, s_im in (
        (0, re_odd, im_odd, spec_re_odd, spec_im_odd),
        (1, re_even, im_even, spec_re_even, spec_im_even),
    ):
        orders = (2 * index + 1 + parity).astype(jnp.float32)
        rate = (nonlinear_gain / overall) * orders
        re_new = re - rate * s_im
        im_new = im + rate * s_re
        total += jnp.sum(orders * (re_new * re_new + im_new * im_new), 0, keepdims=True)
        fresh[0, parity] = re_new
        fresh[1, parity] = im_new
    heat[...] = total
    part = count // harm_count
    for k, out in enumerate(outs):
        at = pl.ds(pl.multiple_of((h ^ k) * part, part), part)
        for c in range(2):
            for parity in range(2):
                out[c, parity] = fresh[c, parity, at, :]


def collect_kernel(parts, where, *refs):
    *blocks, out, stage, sems = refs
    h = where[0]
    height = len(blocks)
    count = blocks[0].shape[2] // parts
    length = 2 * height * count
    writes = []
    for c in range(2):
        for part in range(parts):
            for k, block in enumerate(blocks):
                for parity in range(2):
                    first = part * length + parity * height + (h ^ k)
                    stage[c, pl.ds(first, count, stride=2 * height), :] = block[
                        c, parity, part * count : (part + 1) * count, :
                    ]
            at = slice(part * length, (part + 1) * length)
            write = pltpu.make_async_copy(
                stage.at[c, at], out.at[c, at], sems.at[c * parts + part]
            )
            write.start()
            writes.append(write)
    for write in writes:
        write.wait()


def look_kernel(where, conduct, perfuse, absorb, label, prior, out):
    row = pl.ds(where[0], 1)
    kinds = label[row, :]
    out[0:1, :] = prior[row, :]
    for item, table in ((1, conduct), (2, perfuse), (3, absorb)):
        values = jnp.zeros(kinds.shape, jnp.float32)
        for kind in range(table.shape[0]):
            values = jnp.where(kinds == kind, table[kind], values)
        out[item : item + 1, :] = values


def cast_kernel(overall, maps, heat, out):
    deposit = maps[3:4, :] * heat[...] / (float(overall) * float(overall))
    items = jnp.concatenate([maps[0:3, :], deposit], 0)
    out[...] = jnp.broadcast_to(items[None], out.shape)


def warm_kernel(tx_count, ty_count, where, rows, out, field):
    tx, ty = where[1], where[2]
    height, breadth = out.shape
    items = rows.shape[1]
    lane = lax.broadcasted_iota(jnp.int32, (items, breadth), 1)
    lower = lane < breadth // 2
    side = (lower & (ty < ty_count - 1)) | (~lower & (ty > 0))
    padded = field.shape[1] // items
    field[:, 3 * height * items :, :] = jnp.zeros(
        (2, (padded - 3 * height) * items, breadth), jnp.float32
    )
    for part in range(3):
        row = tx + part - 1
        inside = (row >= 0) & (row < tx_count)
        left, right = jnp.maximum(ty - 1, 0), jnp.minimum(ty + 1, ty_count - 1)
        for r in range(height):
            at = (r * tx_count + jnp.clip(row, 0, tx_count - 1)) * ty_count
            to = slice((part * height + r) * items, (part * height + r + 1) * items)
            past = jnp.where(lower, rows[at + right], rows[at + left])
            field[0, to, :] = jnp.where(inside, rows[at + ty], 0.0)
            field[1, to, :] = jnp.where(inside & side, past, 0.0)

    def item(i):
        return [field[tile, pl.ds(i, padded, stride=items), :] for tile in range(2)]

    (t, tb), conduct, perfuse, deposit = (item(i) for i in range(items))
    lane = lax.broadcasted_iota(jnp.int32, (padded, breadth), 1)
    first, last = lane == 0, lane == breadth - 1
    for _ in range(4):
        m1, b1 = pltpu.roll(t, breadth - 1, 1), pltpu.roll(tb, breadth - 1, 1)
        m2, b2 = pltpu.roll(t, 1, 1), pltpu.roll(tb, 1, 1)
        near = jnp.where(last, b1, m1) + jnp.where(first, b2, m2)
        near_b = jnp.where(last, m1, b1) + jnp.where(first, m2, b2)
        lap = pltpu.roll(t, padded - 1, 0) + pltpu.roll(t, 1, 0) + near - 4.0 * t
        lap_b = pltpu.roll(tb, padded - 1, 0) + pltpu.roll(tb, 1, 0) + near_b - 4.0 * tb
        t = t + conduct[0] * lap - perfuse[0] * t + deposit[0]
        tb = tb + conduct[1] * lap_b - perfuse[1] * tb + deposit[1]
    out[...] = t[height : 2 * height]


def body(
    wave_spectrum,
    lens_window,
    medium_label,
    thermal_excess_prior,
    attenuation_by_kind,
    blood_drain_by_kind,
    diffusivity_by_kind,
):
    _, own, height, breadth = wave_spectrum.shape
    harm_count = lax.axis_size("harm")
    tx_count = lax.axis_size("tx")
    ty_count = lax.axis_size("ty")
    overall = own * harm_count
    assert height == harm_count and CYCLE_READINGS == 4 * overall
    hq = own // tx_count
    rows = height * tx_count
    where = jnp.stack(
        [lax.axis_index("harm"), lax.axis_index("tx"), lax.axis_index("ty")]
    ).astype(jnp.int32)

    small = (height, breadth)
    blocks = call(
        spread_kernel,
        (where, wave_spectrum.reshape(2, own * height, breadth), lens_window),
        [f32(height, 2, hq, breadth)] * tx_count,
        scratch=[
            pltpu.VMEM((2, own * height, breadth), jnp.float32),
            pltpu.VMEM(small, jnp.int32),
            pltpu.SemaphoreType.DMA((3,)),
        ],
        places=[SMEM, HBM, HBM],
    )
    blocks = [blocks[0]] + [swap(blocks[k], "tx", k) for k in range(1, tx_count)]

    tiles = -(-rows * STRIP // breadth)
    plane, strips = call(
        strip_kernel,
        (where, *blocks),
        [f32(rows, 2, hq, breadth), f32(tiles, 2, hq, breadth)],
        places=[SMEM] + [VMEM] * tx_count,
    )
    if ty_count == 2:
        strips = [swap(strips, "ty", 1)]
    else:
        strips = [
            lax.ppermute(strips, "ty", [(i, i + 1) for i in range(ty_count - 1)]),
            lax.ppermute(strips, "ty", [(i + 1, i) for i in range(ty_count - 1)]),
        ]
    owners = harm_count * tx_count
    moved = call(
        functools.partial(bend_kernel, tx_count, ty_count, own),
        (
            where,
            plane,
            jnp.asarray(column_powers(breadth, ty_count), jnp.bfloat16),
            *strips,
        ),
        f32(owners, 2, hq, breadth),
        scratch=[
            pltpu.VMEM((2, rows * hq, ORDER * breadth), jnp.float32),
            pltpu.VMEM((hq // 8, owners, 2, 8, breadth), jnp.float32),
            pltpu.SemaphoreType.DMA((hq // 8,)),
        ],
        places=[SMEM] + [VMEM] * (2 + len(strips)),
        out_specs=HBM,
    )
    pixels = lax.all_to_all(
        moved.reshape(owners, 2 * hq, breadth),
        ("harm", "tx"),
        split_axis=0,
        concat_axis=0,
        tiled=True,
    ).reshape(moved.shape)

    half = overall // 2
    coarse, fine = (jnp.asarray(x) for x in table_seeds(overall))
    table = jax.ShapeDtypeStruct((3, 2, half, half), jnp.bfloat16)
    tables = call(table_kernel, (coarse, fine), [table] * 2)
    maps = call(
        look_kernel,
        (
            where,
            diffusivity_by_kind,
            blood_drain_by_kind,
            attenuation_by_kind,
            medium_label,
            thermal_excess_prior,
        ),
        f32(4, breadth),
        places=[SMEM] * 4 + [VMEM] * 2,
    )
    pixels, maps = lax.optimization_barrier((pixels, maps))
    *fresh, heat = call(
        functools.partial(burgers_kernel, tx_count),
        (where, pixels, *tables),
        [f32(2, 2, own // 2, breadth)] * harm_count + [f32(1, breadth)],
        scratch=[pltpu.VMEM((2, 2, half, breadth), jnp.float32)],
        places=[SMEM] + [VMEM] * 3,
    )
    back = [fresh[0]]
    for k in range(1, harm_count):
        back.append(swap(fresh[k], "harm", k))
    owed = call(
        functools.partial(cast_kernel, overall),
        (maps, heat),
        f32(owners * ty_count, 4, breadth),
        out_specs=VMEM,
    )
    owed = lax.all_to_all(
        owed, ("harm", "tx", "ty"), split_axis=0, concat_axis=0, tiled=True
    )
    parts = 2
    field = call(
        functools.partial(collect_kernel, parts),
        (where, *back),
        f32(2, own * height, breadth),
        scratch=[
            pltpu.VMEM((2, own * height, breadth), jnp.float32),
            pltpu.SemaphoreType.DMA((2 * parts,)),
        ],
        places=[SMEM] + [VMEM] * harm_count,
        out_specs=HBM,
    )
    field, owed = lax.optimization_barrier((field, owed))
    padded = -(-3 * height // 8) * 8
    later = call(
        functools.partial(warm_kernel, tx_count, ty_count),
        (where, owed),
        f32(*small),
        scratch=[pltpu.VMEM((2, 4 * padded, breadth), jnp.float32)],
        places=[SMEM, VMEM],
        out_specs=VMEM,
    )
    return field.reshape(2, own, height, breadth), later


def solution(mesh):
    in_specs = (
        P(None, "harm", "tx", "ty"),
        P("tx", "ty"),
        P("tx", "ty"),
        P("tx", "ty"),
        P(),
        P(),
        P(),
    )
    out_specs = (P(None, "harm", "tx", "ty"), P("tx", "ty"))
    return jax.shard_map(
        body, mesh=mesh, in_specs=in_specs, out_specs=out_specs, check_vma=False
    )
```

```python
import functools
import math

import jax
import jax.numpy as jnp
import numpy as np
from jax import lax
from jax.experimental import pallas as pl
from jax.experimental.pallas import tpu as pltpu
from jax.sharding import PartitionSpec as P

CYCLE_READINGS = 2048
diffraction_gain = 0.3
nonlinear_gain = 0.3
ORDER = 4
STRIP = 2 * ORDER
GRANT = 16 * 2**20

VMEM = pl.BlockSpec(memory_space=pltpu.VMEM)
SMEM = pl.BlockSpec(memory_space=pltpu.SMEM)
HBM = pl.BlockSpec(memory_space=pltpu.HBM)


def call(kernel, args, outs, scratch=(), places=None, out_specs=None):
    places = places or [VMEM] * len(args)
    spaces = {id(VMEM): pltpu.VMEM, id(HBM): pltpu.HBM}
    args = [
        pltpu.with_memory_space_constraint(a, spaces[id(place)]) if id(place) in spaces else a
        for a, place in zip(args, places)
    ]
    if out_specs is None:
        out_specs = jax.tree.map(lambda _: VMEM, outs)
        outs = jax.tree.map(lambda o: pltpu.VMEM(o.shape, o.dtype), outs)
    return pl.pallas_call(
        kernel,
        out_shape=outs,
        in_specs=places,
        out_specs=out_specs,
        scratch_shapes=scratch,
        compiler_params=pltpu.CompilerParams(vmem_limit_bytes=GRANT),
    )(*args)


def f32(*shape):
    return jax.ShapeDtypeStruct(shape, jnp.float32)


def swap(block, axis, k):
    count = lax.axis_size(axis)
    return lax.ppermute(block, axis, [(i, i ^ k) for i in range(count)])


def first_harmonic(h, q, own, hq, half):
    return h * own + 1 + q // half + 2 * lax.rem(q, half) * hq


def spread_kernel(wave, lens, *refs):
    *outs, tile, window, sems = refs
    copies = [
        pltpu.make_async_copy(lens, window, sems.at[0]),
        pltpu.make_async_copy(wave.at[0], tile.at[0], sems.at[1]),
        pltpu.make_async_copy(wave.at[1], tile.at[1], sems.at[2]),
    ]
    for copy in copies:
        copy.start()
    tx = lax.axis_index("tx")
    half = len(outs) // 2
    height, _, hq, _ = outs[0].shape
    copies[0].wait()
    weight = 0.25 + 0.75 * window[...].astype(jnp.float32)
    for c in range(2):
        copies[1 + c].wait()
        for k, out in enumerate(outs):
            q = tx ^ k
            start = (q // half + 2 * lax.rem(q, half) * hq) * height
            for r in range(height):
                rows = tile[c, pl.ds(start + r, hq, stride=2 * height), :]
                out[r, c] = rows * weight[r : r + 1, :]


def pack_kernel(*refs):
    blocks, packs = refs[: len(refs) // 2], refs[len(refs) // 2 :]
    height, _, hq, breadth = blocks[0].shape
    slot = lax.broadcasted_iota(jnp.int32, (8, breadth), 1) // STRIP
    for c in range(2):
        packed = [jnp.zeros((8, breadth), jnp.float32)] * len(blocks)
        for i in range(hq // 8 * height):
            g, r = divmod(i, height)
            for k, block in enumerate(blocks):
                rolled = pltpu.roll(block[r, c, 8 * g : 8 * g + 8, :], STRIP * i + ORDER, 1)
                packed[k] = jnp.where(slot == i, rolled, packed[k])
        for k, pack in enumerate(packs):
            pack[c] = packed[k]


def column_powers(breadth, ty_count):
    kinds = {1: [(1, 1)], 2: [(1, 0), (0, 1)]}.get(ty_count, [(1, 0), (0, 0), (0, 1)])
    wide = breadth + STRIP
    out = []
    for at_left, at_right in kinds:
        step = np.eye(wide, k=1) + np.eye(wide, k=-1) - 2 * np.eye(wide)
        outside = np.zeros(wide, bool)
        outside[:ORDER] = at_left
        outside[wide - ORDER :] = at_right
        step[outside] = 0
        step[:, outside] = 0
        power, powers = np.eye(wide), []
        for _ in range(ORDER):
            power = power @ step
            powers.append(power[:, ORDER : ORDER + breadth])
        powers = np.concatenate(powers, 1)
        past = np.concatenate([powers[:ORDER], powers[wide - ORDER :]])
        out.append(np.concatenate([powers[ORDER : ORDER + breadth], np.tile(past, (breadth // STRIP, 1))]))
    return np.stack(out)


def bend_kernel(tx_count, ty_count, own, powers, *refs):
    blocks, packs = refs[:tx_count], refs[tx_count:-3]
    out, plane, shifted = refs[-3:]
    h, tx, ty = (lax.axis_index(name) for name in ("harm", "tx", "ty"))
    height, _, hq, breadth = blocks[0].shape
    rows = height * tx_count
    lane = lax.broadcasted_iota(jnp.int32, (8, breadth), 1)
    slot = lane // STRIP
    matrix = powers[
        jnp.where(ty == 0, 0, jnp.where(ty == ty_count - 1, powers.shape[0] - 1, 1))
    ]
    along, past = matrix[:breadth], matrix[breadth:]
    right = jnp.concatenate([along, along, past, past], 0)
    for c in range(2):
        inside, beyond = [], []
        for k, block in enumerate(blocks):
            pack = packs[k][c]
            if len(packs) == 2 * tx_count:
                pack = jnp.where(lane % STRIP < ORDER, pack, packs[tx_count + k][c])
            for r in range(height):
                inside.append(block[r, c])
                plane[(tx ^ k) * height + r, c] = block[r, c]
                for g in range(hq // 8):
                    beyond.append(jnp.where(slot == g * height + r, pack, 0.0))
        left = split(jnp.concatenate(inside, 0)) + split(jnp.concatenate(beyond, 0))
        result = jnp.dot(
            jnp.concatenate(left, 1), right, preferred_element_type=jnp.float32
        )
        for k in range(tx_count):
            for r in range(height):
                at = (k * height + r) * hq
                shifted[(tx ^ k) * height + r, c] = result[at : at + hq]
    low = first_harmonic(h, tx, own, hq, tx_count // 2)
    inner = lax.broadcasted_iota(jnp.int32, (8, breadth), 0)
    zero = jnp.zeros((8, breadth), jnp.float32)

    def across(v):
        return [
            ((v[row + 1] if row < rows - 1 else zero) + (v[row - 1] if row else zero))
            - 2.0 * v[row]
            for row in range(rows)
        ]

    def group(g, carry):
        at = pl.multiple_of(g * 8, 8)
        gain = diffraction_gain / (low + 2 * (at + inner)).astype(jnp.float32)

        def power(c, b):
            return [
                shifted[row, c, pl.ds(at, 8), (b - 1) * breadth : b * breadth]
                for row in range(rows)
            ]

        base = [[plane[row, c, pl.ds(at, 8), :] for row in range(rows)] for c in range(2)]
        re, im = base
        factor = gain
        for b, divider in ((1, 4.0), (2, 3.0), (3, 2.0), (4, 1.0)):
            p_re, p_im = power(0, b), power(1, b)
            if b % 4 == 1:
                p_re, p_im, signs = p_im, p_re, (-1.0, 1.0)
            elif b % 4 == 2:
                signs = (-1.0, -1.0)
            elif b % 4 == 3:
                p_re, p_im, signs = p_im, p_re, (1.0, -1.0)
            else:
                signs = (1.0, 1.0)
            base = [
                [v + (signs[c] * factor) * p for v, p in zip(base[c], (p_re, p_im)[c])]
                for c in range(2)
            ]
            factor = factor * gain * (1.0 / (b + 1))
            rate = gain * (1.0 / divider)
            lap_re, lap_im = across(re), across(im)
            re = [v - rate * l for v, l in zip(base[0], lap_im)]
            im = [v + rate * l for v, l in zip(base[1], lap_re)]
        for row in range(rows):
            to = (row % height) * tx_count + row // height
            out[to, 0, pl.ds(at, 8), :] = re[row]
            out[to, 1, pl.ds(at, 8), :] = im[row]
        return carry

    lax.fori_loop(0, hq // 8, group, 0, unroll=True)


def table_seeds(overall):
    half = overall // 2
    unit = np.pi / (2 * overall)
    even = 2 * np.arange(half) + 2
    rows, eight = np.arange(half // 8)[:, None], np.arange(8)[:, None]
    theta = unit * (np.arange(half) + 0.5)
    coarse = [16 * rows * theta, 8 * rows * unit * even, 16 * rows * theta]
    fine = [(2 * eight + 1) * theta, unit * (eight + 0.5) * even, (2 * eight + 2) * theta]
    pair = lambda x: np.stack([np.cos(x), np.sin(x)], 1).astype(np.float32)
    return pair(np.stack(coarse)), pair(np.stack(fine))


def split(x):
    high = x.astype(jnp.bfloat16)
    return high, (x - high.astype(jnp.float32)).astype(jnp.bfloat16)


def table_kernel(coarse, fine, high, low):
    for kind in range(coarse.shape[0]):
        cos_f, sin_f = fine[kind, 0], fine[kind, 1]

        def step(g, carry, kind=kind, cos_f=cos_f, sin_f=sin_f):
            cos_rows, sin_rows = [], []
            for j in range(2):
                cos_c = coarse[kind, 0, pl.ds(2 * g + j, 1), :]
                sin_c = coarse[kind, 1, pl.ds(2 * g + j, 1), :]
                cos_rows.append(cos_c * cos_f - sin_c * sin_f)
                sin_rows.append(sin_c * cos_f + cos_c * sin_f)
            at = pl.ds(pl.multiple_of(g * 16, 16), 16)
            for i, parts in enumerate((cos_rows, sin_rows)):
                h, l = split(jnp.concatenate(parts, 0))
                high[kind, i, at, :] = h
                low[kind, i, at, :] = l
            return carry

        lax.fori_loop(0, high.shape[2] // 16, step, 0)


def product(high, low, kind, i, *columns):
    width = columns[0].shape[1]
    parts = [split(x) for x in columns]
    full = jnp.dot(
        high[kind, i],
        jnp.concatenate([p for pair in parts for p in pair], 1),
        preferred_element_type=jnp.float32,
    )
    rest = jnp.dot(
        low[kind, i],
        jnp.concatenate([pair[0] for pair in parts], 1),
        preferred_element_type=jnp.float32,
    )
    return [
        full[:, 2 * j * width : (2 * j + 1) * width]
        + (
            full[:, (2 * j + 1) * width : (2 * j + 2) * width]
            + rest[:, j * width : (j + 1) * width]
        )
        for j in range(len(columns))
    ]


def burgers_kernel(tx_count, pixels, high, low, *refs):
    *outs, heat, fresh = refs
    h = lax.axis_index("harm")
    _, _, _, breadth = pixels.shape
    harm_count = len(outs)
    half = tx_count // 2
    count = fresh.shape[2]
    overall = 2 * count
    ODD, BY_TIME, BY_ORDER = 0, 1, 2

    def gather(c, parity):
        blocks = [
            pixels[g * tx_count + q, c]
            for g in range(harm_count)
            for q in range(parity * half, (parity + 1) * half)
        ]
        return jnp.concatenate(blocks, 0)

    index = lax.broadcasted_iota(jnp.int32, (count, breadth), 0)
    flip = jnp.where(index % 2 == 0, 1.0, -1.0)
    re_odd, re_even = gather(0, 0), gather(0, 1)
    im_odd, im_even = gather(1, 0), gather(1, 1)
    b0, u1 = product(high, low, ODD, 0, re_odd, flip * im_odd)
    u0, b1 = product(high, low, ODD, 1, im_odd, flip * re_odd)
    a0, a1 = product(high, low, BY_TIME, 0, re_even, -flip * re_even)
    v0, v1 = product(high, low, BY_TIME, 1, im_even, flip * im_even)
    scale = 1.0 / (2 * overall * math.sqrt(overall))
    cos0, sin0 = product(high, low, ODD, 0, a0 * b0 + u0 * v0, a1 * u1 + b1 * v1)
    sin1, cos1 = product(high, low, ODD, 1, a0 * u0 + b0 * v0, a1 * b1 + u1 * v1)
    spec_re_odd = (8.0 * scale) * (cos0 + flip * cos1)
    spec_im_odd = (8.0 * scale) * (sin1 + flip * sin0)
    even0, even1 = product(
        high,
        low,
        BY_ORDER,
        0,
        (a0 * a0 + b0 * b0) + (u0 * u0 + v0 * v0),
        (a1 * a1 + b1 * b1) + (u1 * u1 + v1 * v1),
    )
    spec_re_even = (4.0 * scale) * (even0 - flip * even1)
    even0, even1 = product(
        high, low, BY_ORDER, 1, a0 * v0 + b0 * u0, a1 * v1 + b1 * u1
    )
    spec_im_even = (8.0 * scale) * (even0 + flip * even1)
    total = jnp.zeros((1, breadth), jnp.float32)
    for parity, re, im, s_re, s_im in (
        (0, re_odd, im_odd, spec_re_odd, spec_im_odd),
        (1, re_even, im_even, spec_re_even, spec_im_even),
    ):
        orders = (2 * index + 1 + parity).astype(jnp.float32)
        rate = (nonlinear_gain / overall) * orders
        re_new = re - rate * s_im
        im_new = im + rate * s_re
        total += jnp.sum(orders * (re_new * re_new + im_new * im_new), 0, keepdims=True)
        fresh[0, parity] = re_new
        fresh[1, parity] = im_new
    heat[...] = total
    part = count // harm_count
    for k, out in enumerate(outs):
        at = pl.ds(pl.multiple_of((h ^ k) * part, part), part)
        for c in range(2):
            for parity in range(2):
                out[c, parity] = fresh[c, parity, at, :]


def collect_kernel(parts, *refs):
    *blocks, out, stage, sems = refs
    h = lax.axis_index("harm")
    height = len(blocks)
    count = blocks[0].shape[2] // parts
    length = 2 * height * count
    writes = []
    for c in range(2):
        for part in range(parts):
            for k, block in enumerate(blocks):
                for parity in range(2):
                    first = part * length + parity * height + (h ^ k)
                    stage[c, pl.ds(first, count, stride=2 * height), :] = block[
                        c, parity, part * count : (part + 1) * count, :
                    ]
            at = slice(part * length, (part + 1) * length)
            write = pltpu.make_async_copy(
                stage.at[c, at], out.at[c, at], sems.at[c * parts + part]
            )
            write.start()
            writes.append(write)
    for write in writes:
        write.wait()


def look_kernel(conduct, perfuse, absorb, label, prior, out):
    row = pl.ds(lax.axis_index("harm"), 1)
    kinds = label[row, :]
    out[0:1, :] = prior[row, :]
    for item, table in ((1, conduct), (2, perfuse), (3, absorb)):
        values = jnp.zeros(kinds.shape, jnp.float32)
        for kind in range(table.shape[0]):
            values = jnp.where(kinds == kind, table[kind], values)
        out[item : item + 1, :] = values


def cast_kernel(overall, maps, heat, out):
    deposit = maps[3:4, :] * heat[...] / (float(overall) * float(overall))
    items = jnp.concatenate([maps[0:3, :], deposit], 0)
    out[...] = jnp.broadcast_to(items[None], out.shape)


def warm_kernel(tx_count, ty_count, rows, out, field):
    tx, ty = lax.axis_index("tx"), lax.axis_index("ty")
    height, breadth = out.shape
    items = rows.shape[1]
    lane = lax.broadcasted_iota(jnp.int32, (items, breadth), 1)
    lower = lane < breadth // 2
    side = (lower & (ty < ty_count - 1)) | (~lower & (ty > 0))
    padded = field.shape[1] // items
    field[:, 3 * height * items :, :] = jnp.zeros(
        (2, (padded - 3 * height) * items, breadth), jnp.float32
    )
    for part in range(3):
        row = tx + part - 1
        inside = (row >= 0) & (row < tx_count)
        left, right = jnp.maximum(ty - 1, 0), jnp.minimum(ty + 1, ty_count - 1)
        for r in range(height):
            at = (r * tx_count + jnp.clip(row, 0, tx_count - 1)) * ty_count
            to = slice((part * height + r) * items, (part * height + r + 1) * items)
            past = jnp.where(lower, rows[at + right], rows[at + left])
            field[0, to, :] = jnp.where(inside, rows[at + ty], 0.0)
            field[1, to, :] = jnp.where(inside & side, past, 0.0)

    def item(i):
        return [field[tile, pl.ds(i, padded, stride=items), :] for tile in range(2)]

    (t, tb), conduct, perfuse, deposit = (item(i) for i in range(items))
    lane = lax.broadcasted_iota(jnp.int32, (padded, breadth), 1)
    first, last = lane == 0, lane == breadth - 1
    for _ in range(4):
        m1, b1 = pltpu.roll(t, breadth - 1, 1), pltpu.roll(tb, breadth - 1, 1)
        m2, b2 = pltpu.roll(t, 1, 1), pltpu.roll(tb, 1, 1)
        near = jnp.where(last, b1, m1) + jnp.where(first, b2, m2)
        near_b = jnp.where(last, m1, b1) + jnp.where(first, m2, b2)
        lap = pltpu.roll(t, padded - 1, 0) + pltpu.roll(t, 1, 0) + near - 4.0 * t
        lap_b = pltpu.roll(tb, padded - 1, 0) + pltpu.roll(tb, 1, 0) + near_b - 4.0 * tb
        t = t + conduct[0] * lap - perfuse[0] * t + deposit[0]
        tb = tb + conduct[1] * lap_b - perfuse[1] * tb + deposit[1]
    out[...] = t[height : 2 * height]


def sides(packs):
    tx_count, ty_count = lax.axis_size("tx"), lax.axis_size("ty")
    steps = (1,) if ty_count == 2 else (1, -1)
    out = []
    for step in steps:
        for k, pack in enumerate(packs):
            pairs = []
            for tx in range(tx_count):
                for ty in range(ty_count):
                    to = ty ^ 1 if ty_count == 2 else ty + step
                    if 0 <= to < ty_count:
                        pairs.append((tx * ty_count + ty, (tx ^ k) * ty_count + to))
            out.append(lax.ppermute(pack, ("tx", "ty"), pairs))
    return out


def body(
    wave_spectrum,
    lens_window,
    medium_label,
    thermal_excess_prior,
    attenuation_by_kind,
    blood_drain_by_kind,
    diffusivity_by_kind,
):
    _, own, height, breadth = wave_spectrum.shape
    harm_count = lax.axis_size("harm")
    tx_count = lax.axis_size("tx")
    ty_count = lax.axis_size("ty")
    overall = own * harm_count
    assert height == harm_count and CYCLE_READINGS == 4 * overall
    hq = own // tx_count
    rows = height * tx_count
    small = (height, breadth)
    blocks = call(
        spread_kernel,
        (wave_spectrum.reshape(2, own * height, breadth), lens_window),
        [f32(height, 2, hq, breadth)] * tx_count,
        scratch=[
            pltpu.VMEM((2, own * height, breadth), jnp.float32),
            pltpu.VMEM(small, jnp.int32),
            pltpu.SemaphoreType.DMA((3,)),
        ],
        places=[HBM, HBM],
    )
    assert STRIP * height * hq // 8 <= breadth and hq % 8 == 0
    blocks = list(blocks)
    packs = call(pack_kernel, blocks, [f32(2, 8, breadth)] * tx_count)
    for k in range(1, tx_count):
        blocks[k] = swap(blocks[k], "tx", k)
    packs = sides(packs)
    owners = harm_count * tx_count
    moved = call(
        functools.partial(bend_kernel, tx_count, ty_count, own),
        (
            jnp.asarray(column_powers(breadth, ty_count), jnp.bfloat16),
            *blocks,
            *packs,
        ),
        f32(owners, 2, hq, breadth),
        scratch=[
            pltpu.VMEM((rows, 2, hq, breadth), jnp.float32),
            pltpu.VMEM((rows, 2, hq, ORDER * breadth), jnp.float32),
        ],
        places=[VMEM] * (1 + tx_count + len(packs)),
    )
    pixels = lax.all_to_all(
        moved.reshape(owners, 2 * hq, breadth),
        ("harm", "tx"),
        split_axis=0,
        concat_axis=0,
        tiled=True,
    ).reshape(moved.shape)

    half = overall // 2
    coarse, fine = (jnp.asarray(x) for x in table_seeds(overall))
    table = jax.ShapeDtypeStruct((3, 2, half, half), jnp.bfloat16)
    tables = call(table_kernel, (coarse, fine), [table] * 2)
    maps = call(
        look_kernel,
        (
            diffusivity_by_kind,
            blood_drain_by_kind,
            attenuation_by_kind,
            medium_label,
            thermal_excess_prior,
        ),
        f32(4, breadth),
        places=[SMEM] * 3 + [VMEM] * 2,
    )
    pixels, maps = lax.optimization_barrier((pixels, maps))
    *fresh, heat = call(
        functools.partial(burgers_kernel, tx_count),
        (pixels, *tables),
        [f32(2, 2, own // 2, breadth)] * harm_count + [f32(1, breadth)],
        scratch=[pltpu.VMEM((2, 2, half, breadth), jnp.float32)],
        places=[VMEM] * 3,
    )
    back = [fresh[0]]
    for k in range(1, harm_count):
        back.append(swap(fresh[k], "harm", k))
    owed = call(
        functools.partial(cast_kernel, overall),
        (maps, heat),
        f32(owners * ty_count, 4, breadth),
        out_specs=VMEM,
    )
    owed = lax.all_to_all(
        owed, ("harm", "tx", "ty"), split_axis=0, concat_axis=0, tiled=True
    )
    parts = 1
    field = call(
        functools.partial(collect_kernel, parts),
        back,
        f32(2, own * height, breadth),
        scratch=[
            pltpu.VMEM((2, own * height, breadth), jnp.float32),
            pltpu.SemaphoreType.DMA((2 * parts,)),
        ],
        places=[VMEM] * harm_count,
        out_specs=HBM,
    )
    field, owed = lax.optimization_barrier((field, owed))
    padded = -(-3 * height // 8) * 8
    later = call(
        functools.partial(warm_kernel, tx_count, ty_count),
        (owed,),
        f32(*small),
        scratch=[pltpu.VMEM((2, 4 * padded, breadth), jnp.float32)],
        places=[VMEM],
        out_specs=VMEM,
    )
    return field.reshape(2, own, height, breadth), later


def solution(mesh):
    in_specs = (
        P(None, "harm", "tx", "ty"),
        P("tx", "ty"),
        P("tx", "ty"),
        P("tx", "ty"),
        P(),
        P(),
        P(),
    )
    out_specs = (P(None, "harm", "tx", "ty"), P("tx", "ty"))
    return jax.shard_map(body, mesh=mesh, in_specs=in_specs, out_specs=out_specs, check_vma=False)
```
